32 devices in a mesh: seq: 8 (over y, x, core), hid: 4 (over z).
Axes of the slice: x: 2, y: 2, z: 4, core: 2. Of those that a mesh axis runs over, the one named last changes fastest.
Arguments:
- projected: bfloat16 [2048, 3, 4096], P('seq', None, 'hid'), may hold values from -6 to 6
- short_taps: float32 [3, 3, 4096], P(None, None, 'hid'), may hold values from -3 to 3
- long_taps: bfloat16 [4096, 128], P('hid'), may hold values from -0.5 to 0.5
- skip_gain: float32 [4096], P('hid'), may hold values from 0.5 to 2
- out_weight: bfloat16 [4096, 4096], P('hid'), may hold values from -0.09375 to 0.09375
Outputs:
- mixer_out: bfloat16 [2048, 4096], P('seq', 'hid')
The draws below stay inside these ranges and needn't reach their ends.
All inputs are finite; a program needn't handle non-finite values.
Results may differ from the reference program's by a relative error of at most 0.0095.
Values may be sent and summed in bfloat16 or wider, within the bound.
No kernel may reach another device: no remote copies, remote signals or barrier semaphores. Data moves between devices by JAX's collectives and lax.ppermute only.
A program may use at most 64 MiB of HBM per device.

```python
import math
import jax
import jax.numpy as jnp
from jax import lax

CH = 4096
OUTW = 4096
FLEN = 128
TOKENS = 2048
N_HID = 4


def level_of(stream_key, shape, split, smallest, largest):
    def one(position, blocks):
        heights = jax.random.uniform(jax.random.fold_in(jax.random.fold_in(stream_key, 6), position), (blocks,), jnp.float32, smallest / len(split), largest / len(split))
        return jnp.repeat(jnp.exp(heights), shape[position] // blocks).reshape((-1,) + (1,) * (len(shape) - position - 1))

    level = one(*split[0])
    for cut in split[1:]:
        level = level * one(*cut)
    return level


def normal_values(own_key, extent, scale, bound, pieces=(), held_as=jnp.bfloat16):
    values = scale * jax.random.normal(own_key, extent, jnp.float32)
    if pieces:
        values = values * level_of(own_key, extent, pieces, -0.22, 0.18)
    return jnp.clip(values, -bound, bound).astype(held_as)


def setup_inputs(seed: int = 0) -> dict:
    keys = jax.random.split(jax.random.key(seed), 6)
    projected = normal_values(keys[0], (TOKENS, 3, CH), 1.0, 6.0, ((0, 8), (2, 4)))
    short_taps = normal_values(keys[1], (3, 3, CH), 0.6, 3.0, ((2, 4),), jnp.float32)
    long_taps = normal_values(keys[2], (CH, FLEN), FLEN ** -0.5, 0.5, ((0, 4),))
    skip_gain = jnp.clip(jnp.exp(math.log(2.0) - 1.3862944 * jax.random.uniform(keys[3], (CH,), jnp.float32) ** level_of(keys[3], (CH,), ((0, 4),), -0.2, 0.2)), 0.5, 2.0)
    out_weight = normal_values(keys[4], (CH, OUTW), CH ** -0.5, 0.09375, ((0, 4),))
    return {"projected": projected, "short_taps": short_taps, "long_taps": long_taps, "skip_gain": skip_gain, "out_weight": out_weight}


def short_filter(ext, taps):
    first = ext[2:].astype(jnp.float32)
    second = ext[1:-1].astype(jnp.float32)
    third = ext[:-2].astype(jnp.float32)
    return taps[0] * first + taps[1] * second + taps[2] * third


def toeplitz(taps):
    groups, length = taps.shape
    padded = jnp.concatenate([jnp.zeros((groups, length + 1), taps.dtype), taps[:, ::-1], jnp.zeros((groups, length - 1), taps.dtype)], axis=1)
    flat = jnp.tile(padded, (1, length))
    cut = flat[:, length:length + length * (3 * length - 1)].reshape(groups, length, 3 * length - 1)
    return cut[:, :, :2 * length]


def filter_blocks(windows, taps, group):
    channels = taps.shape[0]
    count = channels // group

    def one(index):
        part_taps = lax.dynamic_slice_in_dim(taps, index * group, group, 0)
        part_win = lax.dynamic_slice_in_dim(windows, index * group, group, 2)
        matrix = toeplitz(part_taps).astype(jnp.float32)
        return jnp.einsum("gis,nsg->nig", matrix, part_win.astype(jnp.float32))

    stacked = lax.map(one, jnp.arange(count, dtype=jnp.int32))
    blocks = stacked.shape[1]
    length = stacked.shape[2]
    return jnp.transpose(stacked, (1, 2, 0, 3)).reshape(blocks * length, channels)


def reference(projected, short_taps, long_taps, skip_gain, out_weight):
    tokens = projected.shape[0]
    channels = projected.shape[2]
    length = long_taps.shape[1]
    ext = jnp.concatenate([jnp.zeros((2, 3, channels), projected.dtype), projected], axis=0)
    feat = short_filter(ext, short_taps)
    gated = (feat[:, 1] * feat[:, 2]).astype(jnp.bfloat16)
    padded = jnp.concatenate([jnp.zeros((length, channels), jnp.bfloat16), gated], axis=0)
    blocks = padded.reshape(tokens // length + 1, length, channels)
    windows = jnp.concatenate([blocks[:-1], blocks[1:]], axis=1)
    group = 64 if channels % 64 == 0 else channels
    filtered = filter_blocks(windows, long_taps, group) + skip_gain * gated.astype(jnp.float32)
    mixed = (feat[:, 0] * filtered).astype(jnp.bfloat16)
    width = channels // N_HID
    total = jnp.zeros((tokens, out_weight.shape[1]), jnp.float32)
    for index in range(N_HID):
        partial_sum = jnp.dot(mixed[:, index * width:(index + 1) * width], out_weight[index * width:(index + 1) * width], preferred_element_type=jnp.float32)
        total = total + partial_sum.astype(jnp.bfloat16).astype(jnp.float32)
    return total.astype(jnp.bfloat16)
```

```python
import functools

import jax
import jax.numpy as jnp
import numpy as np
from jax import lax
from jax.experimental import pallas as pl
from jax.experimental.pallas import tpu as pltpu
from jax.sharding import PartitionSpec as P

F32 = jnp.float32
BF16 = jnp.bfloat16
PAD = 16
STRIP = 256
ANY = pl.BlockSpec(memory_space=pl.ANY)


def split(values):
    high = values.astype(BF16)
    return high, (values - high.astype(F32)).astype(BF16)


def transforms(length):
    size = 2 * length
    angle = np.pi * (2 * np.arange(length)[:, None] + 1) * np.arange(size)[None] / size
    forward = np.concatenate([np.cos(angle), -np.sin(angle)]).astype(np.float32)
    inverse = np.concatenate([np.cos(angle), -np.sin(angle)]).T[length:] / length

    def halves(matrix):
        high = matrix.astype(BF16)
        return high, (matrix - high.astype(np.float64)).astype(BF16)

    return halves(forward.astype(np.float64)) + halves(inverse)


def matmul(a, b):
    return jnp.dot(a, b, preferred_element_type=F32)


def short_filter(ext, taps, rows):
    total = ext.shape[0]
    one = pltpu.roll(ext, 1, 0)
    two = pltpu.roll(ext, 2, 0)
    out = taps[0:1] * ext + taps[1:2] * one + taps[2:3] * two
    return out[total - rows :]


def spectrum_product(x, h):
    half = x.shape[0] // 2
    xr, xi, hr, hi = x[:half], x[half:], h[:half], h[half:]
    return jnp.concatenate([xr * hr - xi * hi, xr * hi + xi * hr])


def filter_window(window, h, fwd_hi, fwd_lo, inv_hi, inv_lo):
    x = matmul(fwd_hi, window) + matmul(fwd_lo, window)
    high, low = split(spectrum_product(x, h))
    return matmul(inv_hi, high) + matmul(inv_lo, high) + matmul(inv_hi, low)


def load_all(pairs, sems):
    copies = [pltpu.make_async_copy(src, dst, sems.at[i]) for i, (src, dst) in enumerate(pairs)]
    for copy in copies:
        copy.start()
    return copies


def column_block(weight, which, width):
    return weight.at[:, pl.ds(pl.multiple_of(which * width, width), width)]


def first_kernel(
    rows, width, proj, short, long_taps, skip, fh, fl, ih, il, weight,
    payload, mixed_out, gated_out, halo_out, h_out,
    k_buf, v_buf, q_buf, short_buf, long_buf, skip_buf, fh_buf, fl_buf, ih_buf, il_buf, w_buf, g_buf, m_buf, sems,
):
    me = lax.axis_index("hid")
    tokens, channels = k_buf.shape
    length = long_buf.shape[1]
    start = tokens - rows - PAD
    copies = load_all(
        [
            (short, short_buf), (proj.at[1], k_buf), (proj.at[2], v_buf), (fh, fh_buf), (fl, fl_buf),
            (long_taps, long_buf), (skip, skip_buf), (proj.at[0, start:], q_buf), (ih, ih_buf), (il, il_buf),
            (column_block(weight, me ^ 3, width), w_buf.at[0]), (column_block(weight, me ^ 1, width), w_buf.at[1]),
        ],
        sems,
    )
    for copy in copies[:10]:
        copy.wait()
    row = lax.broadcasted_iota(jnp.int32, (tokens, STRIP), 0)
    inv_hi = ih_buf[length - rows :]
    inv_lo = il_buf[length - rows :]
    for at in range(0, channels, STRIP):
        part = slice(at, at + STRIP)
        key = short_filter(k_buf[:, part].astype(F32), short_buf[:, 1, part], tokens)
        value = short_filter(v_buf[:, part].astype(F32), short_buf[:, 2, part], tokens)
        gated = jnp.where(row < 2, 0.0, key * value).astype(BF16)
        g_buf[:, part] = gated
        taps = long_buf[part]
        contract = (((1,), (1,)), ((), ()))
        h = lax.dot_general(fh_buf[:, :length], taps, contract, preferred_element_type=F32)
        h += lax.dot_general(fl_buf[:, :length], taps, contract, preferred_element_type=F32)
        h = jnp.concatenate([h[:length] + skip_buf[:, part], h[length:]])
        h_out[:, part] = h
        filtered = filter_window(gated, h, fh_buf[...], fl_buf[...], inv_hi, inv_lo)
        query = short_filter(q_buf[:, part].astype(F32), short_buf[:, 0, part], rows)
        m_buf[:, part] = (query * filtered).astype(BF16)
    gated_out[...] = g_buf[...]
    mixed_out[...] = m_buf[...]
    halo_out[:length] = g_buf[tokens - length :]
    halo_out[length : length + PAD] = q_buf[rows:]
    halo_out[length + PAD : length + 2 * PAD] = k_buf[tokens - PAD :]
    halo_out[length + 2 * PAD :] = v_buf[tokens - PAD :]
    for which in range(2):
        copies[10 + which].wait()
        payload[which] = matmul(m_buf[...], w_buf[which]).astype(BF16)


def later_kernel(
    begin, rows, back, width, proj, short, gated, halo, h, fh, fl, ih, il, weight,
    payload, mixed_out,
    head_buf, q_buf, short_buf, gated_buf, halo_buf, h_buf, fh_buf, fl_buf, ih_buf, il_buf, w_buf, m_buf, sems,
):
    me = lax.axis_index("hid")
    length, channels = halo_buf.shape[0] - 3 * PAD, halo_buf.shape[1]
    ahead = 2 * length - back
    low = begin - PAD if begin else 0
    copies = load_all(
        [
            (halo, halo_buf), (short, short_buf), (gated.at[:ahead], gated_buf), (proj.at[1:, :PAD], head_buf),
            (proj.at[0, low : begin + rows], q_buf), (h, h_buf), (fh, fh_buf), (fl, fl_buf), (ih, ih_buf), (il, il_buf),
            (column_block(weight, me ^ 3, width), w_buf.at[0]), (column_block(weight, me ^ 1, width), w_buf.at[1]),
        ],
        sems,
    )
    for copy in copies[:10]:
        copy.wait()
    first = begin + back - length
    inv_hi = ih_buf[first : first + rows]
    inv_lo = il_buf[first : first + rows]
    for at in range(0, channels, STRIP):
        part = slice(at, at + STRIP)

        def head(which, own):
            before = halo_buf[length + which * PAD : length + (which + 1) * PAD, part].astype(F32)
            return jnp.concatenate([before, own.astype(F32)])

        key = short_filter(head(1, head_buf[0, :, part]), short_buf[:, 1, part], PAD)
        value = short_filter(head(2, head_buf[1, :, part]), short_buf[:, 2, part], PAD)
        fixed = (key * value).astype(BF16)
        window = jnp.concatenate([halo_buf[length - back : length, part], fixed, gated_buf[PAD:, part]])
        filtered = filter_window(window, h_buf[:, part], fh_buf[...], fl_buf[...], inv_hi, inv_lo)
        ext = q_buf[:, part].astype(F32) if begin else head(0, q_buf[:, part])
        query = short_filter(ext, short_buf[:, 0, part], rows)
        m_buf[:, part] = (query * filtered).astype(BF16)
    mixed_out[...] = m_buf[...]
    for which in range(2):
        copies[10 + which].wait()
        payload[which] = matmul(m_buf[...], w_buf[which]).astype(BF16)


def keep_kernel(width, mixed, weight, out, w_buf, sems):
    me = lax.axis_index("hid")
    copies = load_all(
        [(column_block(weight, me ^ 2, width), w_buf.at[0]), (column_block(weight, me, width), w_buf.at[1])], sems
    )
    for which in range(2):
        copies[which].wait()
        out[which] = matmul(mixed[...], w_buf[which]).astype(BF16)


def shape(dims, dtype=BF16):
    return jax.ShapeDtypeStruct(dims, dtype)


def swapped(array, axis, mask):
    return lax.ppermute(array, axis, [(i, i ^ mask) for i in range(lax.axis_size(axis))])


def shards(projected, short_taps, long_taps, skip_gain, out_weight):
    tokens, _, channels = projected.shape
    length = long_taps.shape[1]
    width = out_weight.shape[1] // lax.axis_size("hid")
    proj = jnp.transpose(projected, (1, 0, 2))
    consts = [jnp.asarray(m) for m in transforms(length)]
    size = 2 * length
    const_bufs = [pltpu.VMEM(m.shape, BF16) for m in consts]
    w_bufs = pltpu.VMEM((2, channels, width), BF16)
    short_bufs = pltpu.VMEM(short_taps.shape, F32)
    halo_rows = length + 3 * PAD
    rows1 = tokens - length - PAD
    rows3 = length // 2
    rows2 = tokens - rows1 - rows3
    params = pltpu.CompilerParams(vmem_limit_bytes=56 << 20)

    pay1, mixed1, gated, halo, h = pl.pallas_call(
        functools.partial(first_kernel, rows1, width),
        name="first",
        out_shape=(
            shape((2, rows1, width)), shape((rows1, channels)), shape((tokens, channels)),
            shape((halo_rows, channels)), shape((size, channels), F32),
        ),
        in_specs=[ANY] * 9,
        scratch_shapes=[
            pltpu.VMEM((tokens, channels), BF16), pltpu.VMEM((tokens, channels), BF16),
            pltpu.VMEM((rows1 + PAD, channels), BF16), short_bufs, pltpu.VMEM((channels, length), BF16),
            pltpu.VMEM((1, channels), F32), *const_bufs, w_bufs,
            pltpu.VMEM((tokens, channels), BF16), pltpu.VMEM((rows1, channels), BF16), pltpu.SemaphoreType.DMA((12,)),
        ],
        compiler_params=params,
    )(proj, short_taps, long_taps, skip_gain[None], *consts, out_weight)

    got1 = swapped(pay1, "hid", 1)
    span = lax.axis_size("seq")
    before = lax.ppermute(halo, "seq", [(i, i + 1) for i in range(span - 1)])

    def later(begin, rows, back):
        q_rows = rows + PAD if begin else rows
        return pl.pallas_call(
            functools.partial(later_kernel, begin, rows, back, width),
            name=f"later{begin}",
            out_shape=(shape((2, rows, width)), shape((rows, channels))),
            in_specs=[ANY] * 10,
            scratch_shapes=[
                pltpu.VMEM((2, PAD, channels), BF16), pltpu.VMEM((q_rows, channels), BF16), short_bufs,
                pltpu.VMEM((size - back, channels), BF16), pltpu.VMEM((halo_rows, channels), BF16),
                pltpu.VMEM((size, channels), F32), *const_bufs, w_bufs,
                pltpu.VMEM((rows, channels), BF16), pltpu.SemaphoreType.DMA((12,)),
            ],
            compiler_params=params,
        )(proj, short_taps, gated, before, h, *consts, out_weight)

    def keep(mixed):
        return pl.pallas_call(
            functools.partial(keep_kernel, width),
            name="keep",
            out_shape=shape((2, mixed.shape[0], width)),
            in_specs=[pl.BlockSpec(memory_space=pltpu.VMEM), ANY],
            scratch_shapes=[w_bufs, pltpu.SemaphoreType.DMA((2,))],
            compiler_params=params,
        )(mixed, out_weight)

    pay2, mixed2 = later(rows3, rows2, length - PAD)
    got2 = swapped(pay2, "hid", 1)
    pay3, mixed3 = later(0, rows3, length)
    got3 = swapped(pay3, "hid", 1)

    def total(a, b):
        return (a.astype(F32) + b.astype(F32)).astype(BF16)

    pieces = []
    for got, mixed in ((got1, mixed1), (got2, mixed2), (got3, mixed3)):
        mine = keep(mixed)
        there = swapped(total(got[0], mine[0]), "hid", 2)
        pieces.append((got[1].astype(F32) + mine[1].astype(F32) + there.astype(F32)).astype(BF16))
    return jnp.concatenate(pieces[::-1])


def solution(mesh):
    placed = (P("seq", None, "hid"), P(None, None, "hid"), P("hid", None), P("hid"), P("hid", None))
    return jax.shard_map(
        shards, mesh=mesh, in_specs=placed, out_specs=P("seq", "hid"), check_vma=False
    )
```

```python
import functools

import jax
import jax.numpy as jnp
import numpy as np
from jax import lax
from jax.experimental import pallas as pl
from jax.experimental.pallas import tpu as pltpu
from jax.sharding import PartitionSpec as P


F32 = jnp.float32
BF16 = jnp.bfloat16
PAD = 16
STRIP = 256
LAST = 64
VMEM_LIMIT = 40 << 20
LAST = 64
VMEM_LIMIT = 40 << 20
ANY = pl.BlockSpec(memory_space=pl.ANY)
VMEM = pl.BlockSpec(memory_space=pltpu.VMEM)
VMEM = pl.BlockSpec(memory_space=pltpu.VMEM)


def split(values):
    high = values.astype(BF16)
    return high, (values - high.astype(F32)).astype(BF16)


def transforms(length):
    size = 2 * length
    angle = np.pi * (2 * np.arange(length)[:, None] + 1) * np.arange(size)[None] / size
    forward = np.concatenate([np.cos(angle), -np.sin(angle)])
    inverse = forward.T[length:] / length

    def halves(matrix):
        high = matrix.astype(BF16)
        return jnp.asarray(np.concatenate([high, (matrix - high.astype(np.float64)).astype(BF16)]))

    return halves(forward), halves(inverse)


def matmul(a, b):
    return jnp.dot(a, b, preferred_element_type=F32)


def short_filter(ext, taps, rows):
    total = ext.shape[0]
    one = pltpu.roll(ext, 1, 0)
    two = pltpu.roll(ext, 2, 0)
    out = taps[0:1] * ext + taps[1:2] * one + taps[2:3] * two
    return out[total - rows :]


def spectrum_product(x, h):
    half = x.shape[0] // 2
    xr, xi, hr, hi = x[:half], x[half:], h[:half], h[half:]
    return jnp.concatenate([xr * hr - xi * hi, xr * hi + xi * hr])


def both(stacked):
    half = stacked.shape[0] // 2
    return stacked[:half] + stacked[half:]


def filter_window(window, h, fwd, inv, first, rows):
    length = inv.shape[0] // 2
    high, low = split(spectrum_product(both(matmul(fwd[...], window)), h))
    inv_hi = inv[first : first + rows]
    inv_lo = inv[length + first : length + first + rows]
    return both(matmul(jnp.concatenate([inv_hi, inv_lo]), high)) + matmul(inv_hi, low)


def columns(ref, which, width):
    return ref[:, pl.ds(pl.multiple_of(which * width, width), width)]


def first_kernel(
    rows, width, proj_hbm, short_hbm, long_hbm, skip_hbm, fwd_hbm, inv_hbm, w_hbm,
    pay, mixed, gated, halo, h, q, head, short, fwd, inv, w,
    k_buf, v_buf, long_buf, skip_buf, sems,
):
    me = lax.axis_index("hid")
    tokens, channels = k_buf.shape
    length = long_buf.shape[1]
    pairs = [
        (short_hbm, short), (proj_hbm.at[1], k_buf), (proj_hbm.at[2], v_buf), (fwd_hbm, fwd), (long_hbm, long_buf),
        (skip_hbm, skip_buf), (proj_hbm.at[0], q), (inv_hbm, inv), (w_hbm, w),
    ]
    copies = [pltpu.make_async_copy(src, dst, sems.at[i]) for i, (src, dst) in enumerate(pairs)]
    for copy in copies:
        copy.start()
    for copy in copies[:-1]:
        copy.wait()
    row = lax.broadcasted_iota(jnp.int32, (tokens, STRIP), 0)
    for at in range(0, channels, STRIP):
        part = slice(at, at + STRIP)
        key = short_filter(k_buf[:, part].astype(F32), short[:, 1, part], tokens)
        value = short_filter(v_buf[:, part].astype(F32), short[:, 2, part], tokens)
        window = jnp.where(row < 2, 0.0, key * value).astype(BF16)
        gated[:, part] = window
        contract = (((1,), (1,)), ((), ()))
        taps = both(lax.dot_general(fwd[:, :length], long_buf[part], contract, preferred_element_type=F32))
        spectrum = jnp.concatenate([taps[:length] + skip_buf[:, part], taps[length:]])
        h[:, part] = spectrum
        filtered = filter_window(window, spectrum, fwd, inv, length - rows, rows)
        query = short_filter(q[tokens - rows - PAD :, part].astype(F32), short[:, 0, part], rows)
        mixed[:, part] = (query * filtered).astype(BF16)
    halo[:length] = gated[tokens - length :]
    halo[length : length + PAD] = q[tokens - PAD :]
    halo[length + PAD : length + 2 * PAD] = k_buf[tokens - PAD :]
    halo[length + 2 * PAD :] = v_buf[tokens - PAD :]
    head[0] = k_buf[:PAD]
    head[1] = v_buf[:PAD]
    copies[-1].wait()
    pay[0] = matmul(mixed[...], columns(w, me ^ 3, width)).astype(BF16)
    pay[1] = matmul(mixed[...], columns(w, me ^ 1, width)).astype(BF16)


def later_kernel(begin, rows, back, width, halo, gated, h, q, head, short, fwd, inv, w, pay, mixed):
    me = lax.axis_index("hid")
    length, channels = halo.shape[0] - 3 * PAD, halo.shape[1]
    for at in range(0, channels, STRIP):
        part = slice(at, at + STRIP)

        def led(which, own):
            before = halo[length + which * PAD : length + (which + 1) * PAD, part].astype(F32)
            return jnp.concatenate([before, own.astype(F32)])

        key = short_filter(led(1, head[0, :, part]), short[:, 1, part], PAD)
        value = short_filter(led(2, head[1, :, part]), short[:, 2, part], PAD)
        fixed = (key * value).astype(BF16)
        window = jnp.concatenate([halo[length - back : length, part], fixed, gated[PAD : 2 * length - back, part]])
        filtered = filter_window(window, h[:, part], fwd, inv, begin + back - length, rows)
        if begin:
            ext = q[begin - PAD : begin + rows, part].astype(F32)
        else:
            ext = led(0, q[:rows, part])
        query = short_filter(ext, short[:, 0, part], rows)
        mixed[:, part] = (query * filtered).astype(BF16)
    pay[0] = matmul(mixed[...], columns(w, me ^ 3, width)).astype(BF16)
    pay[1] = matmul(mixed[...], columns(w, me ^ 1, width)).astype(BF16)


def keep_kernel(width, count, *refs):
    me = lax.axis_index("hid")
    mixed, w, outs = refs[:count], refs[count], refs[count + 1 :]
    rows = jnp.concatenate([m[...] for m in mixed]) if count > 1 else mixed[0][...]
    for slot, which in ((0, me ^ 2), (1, me)):
        result = matmul(rows, columns(w, which, width)).astype(BF16)
        at = 0
        for out in outs:
            out[slot] = result[at : at + out.shape[1]]
            at += out.shape[1]


def call(kernel, outs, args, in_specs=None, scratch=()):
    if in_specs is None:
        in_specs = [VMEM] * len(args)
        args = [pltpu.with_memory_space_constraint(a, pltpu.VMEM) for a in args]
    return pl.pallas_call(
        kernel,
        out_shape=tuple(pltpu.VMEM(dims, dtype) for dims, dtype in outs),
        in_specs=in_specs,
        out_specs=(VMEM,) * len(outs),
        scratch_shapes=scratch,
        compiler_params=pltpu.CompilerParams(vmem_limit_bytes=VMEM_LIMIT),
    )(*args)


def swapped(array, mask):
    return lax.ppermute(array, "hid", [(i, i ^ mask) for i in range(lax.axis_size("hid"))])


def total(a, b):
    return (a.astype(F32) + b.astype(F32)).astype(BF16)


def mixer(projected, short_taps, long_taps, skip_gain, out_weight):
    tokens, _, channels = projected.shape
    length = long_taps.shape[1]
    width = out_weight.shape[1] // lax.axis_size("hid")
    proj = jnp.transpose(projected, (1, 0, 2))
    fwd, inv = transforms(length)
    size = 2 * length
    rows1 = tokens - length - PAD
    rows3 = LAST
    rows2 = tokens - rows1 - rows3

    pay1, mixed1, gated, halo, h, q, head, short, fwd, inv, w = call(
        functools.partial(first_kernel, rows1, width),
        [
            ((2, rows1, width), BF16), ((rows1, channels), BF16), ((tokens, channels), BF16),
            ((length + 3 * PAD, channels), BF16), ((size, channels), F32), ((tokens, channels), BF16),
            ((2, PAD, channels), BF16), (short_taps.shape, F32), (fwd.shape, BF16), (inv.shape, BF16),
            (out_weight.shape, BF16),
        ],
        [
            pltpu.with_memory_space_constraint(a, pltpu.HBM)
            for a in (proj, short_taps, long_taps, skip_gain[None], fwd, inv, out_weight)
        ],
        [ANY] * 7,
        [
            pltpu.VMEM((tokens, channels), BF16), pltpu.VMEM((tokens, channels), BF16),
            pltpu.VMEM(long_taps.shape, BF16), pltpu.VMEM((1, channels), F32), pltpu.SemaphoreType.DMA((9,)),
        ],
    )
    got1 = swapped(pay1, 1)
    before = lax.ppermute(halo, "seq", [(i, i + 1) for i in range(lax.axis_size("seq") - 1)])

    def later(begin, rows, back):
        return call(
            functools.partial(later_kernel, begin, rows, back, width),
            [((2, rows, width), BF16), ((rows, channels), BF16)],
            (before, gated, h, q, head, short, fwd, inv, w),
        )

    def keep(*mixed):
        return call(
            functools.partial(keep_kernel, width, len(mixed)),
            [((2, m.shape[0], width), BF16) for m in mixed],
            (*mixed, w),
        )

    (keep1,) = keep(mixed1)
    pay2, mixed2 = later(rows3, rows2, length - PAD)
    got2 = swapped(pay2, 1)
    pay3, mixed3 = later(0, rows3, length)
    got3 = swapped(pay3, 1)
    keep2, keep3 = keep(mixed2, mixed3)

    pieces = []
    for got, mine in ((got1, keep1), (got2, keep2), (got3, keep3)):
        there = swapped(total(got[0], mine[0]), 2)
        pieces.append((got[1].astype(F32) + mine[1].astype(F32) + there.astype(F32)).astype(BF16))
    return jnp.concatenate(pieces[::-1])


def solution(mesh):
    placed = (P("seq", None, "hid"), P(None, None, "hid"), P("hid", None), P("hid"), P("hid", None))
    return jax.shard_map(mixer, mesh=mesh, in_specs=placed, out_specs=P("seq", "hid"), check_vma=False)
```
